512 devices in a mesh: row: 128 (over z_hi, y, x, core), col: 4 (over z_lo).
Axes of the slice: x: 4, y: 4, z: 16 (z_hi: 4, z_lo: 4; z = z_hi * 4 + z_lo), core: 2. Of those that a mesh axis runs over, the one named last changes fastest.
Arguments:
- image_tokens: bfloat16 [128, 1024, 1536], P('row', 'col'), may hold values from -60 to 60
- latent: float32 [128, 1024, 64], P('row', 'col'), may hold values from -6 to 6
- text_memory: bfloat16 [128, 2, 154, 768], P('row', None, None, 'col'), may hold values from -500 to 500
- text_len: int32 [128], P('row'), may hold values from 2 to 154, as said below
- timestep: int32 [128], P('row'), may hold values from 1 to 28
- modulation: float32 [128, 5, 1536], P('row'), may hold values from -3 to 3
- projection: bfloat16 [3, 1536, 768], P(None, None, 'col'), may hold values from -0.21875 to 0.21875
- out_weight: bfloat16 [768, 1536], P('col'), may hold values from -0.625 to 0.625
- final_weight: bfloat16 [1536, 64], replicated, may hold values from -0.15625 to 0.15625
Outputs:
- velocity: float32 [128, 1024, 64], P('row', 'col')
- latent_next: float32 [128, 1024, 64], P('row', 'col')
The draws below stay inside these ranges and needn't reach their ends.
Inputs may be any that keep to these rules, and one draw needn't show every extreme that they name: Text keys at positions text_len and beyond take no part; one request has all 154 text tokens valid.
All inputs are finite; a program needn't handle non-finite values.
Results may differ from the reference program's by a relative error of at most 0.012.
The reference program's roundings to bfloat16 on the way count: a program that leaves them out, or rounds other values in their place, can miss the bound.
Values may be sent and summed in bfloat16 or wider, within the bound.
A program may use at most 64 MiB of HBM per device.

```python
import math
import jax
import jax.numpy as jnp
from jax import lax

D = 1536
HEAD = 64
PC = 64
HEADS = 12
TXT = 154
NSTEPS = 28
HD = 768
IMG = 1024
REQ = 128


def draw_image_tokens(key, part):
    base_key, row_key, col_key = jax.random.split(key, 3)
    base = jnp.clip(jax.random.normal(base_key, (REQ, IMG, D), jnp.float32), -5.0, 5.0)
    row_scale = jnp.exp(jax.random.uniform(row_key, (REQ, IMG, 1), jnp.float32, math.log(0.3), math.log(3.0)))
    col_scale = jnp.exp(jax.random.uniform(col_key, (1, 1, D), jnp.float32, math.log(0.3), math.log(3.0)))
    return (base * row_scale * col_scale).astype(jnp.bfloat16)


def draw_text_memory(key, part):
    base_key = jax.random.fold_in(key, 0)
    base = 1.5 * jnp.clip(jax.random.normal(base_key, (REQ, 2, TXT, HEADS * HEAD), jnp.float32), -5.0, 5.0)
    return base.astype(jnp.bfloat16)


def draw_text_len(key, part):
    length_key, pick_key = jax.random.split(key)
    lengths = jax.random.randint(length_key, (REQ,), 2, TXT + 1)
    chosen = jax.random.randint(pick_key, (), 0, REQ)
    positions = jnp.arange(REQ)
    lengths = jnp.where(positions == chosen, TXT, lengths)
    lengths = jnp.where(positions == (chosen + 1) % REQ, 2, lengths)
    return lengths.astype(jnp.int32)


def touch_ends(values, stream_key, smallest, largest):
    spot = [jax.random.randint(jax.random.fold_in(stream_key, axis), (), 0, length) for axis, length in enumerate(values.shape)]
    longest = values.shape.index(max(values.shape))
    beside = spot[:longest] + [(spot[longest] + 1) % values.shape[longest]] + spot[longest + 1:]
    return values.at[tuple(spot)].set(smallest).at[tuple(beside)].set(largest)


def shard_levels(stream_key, extent, shards, smallest, largest):
    def one(position, parts):
        steps = jax.random.uniform(jax.random.fold_in(jax.random.fold_in(stream_key, 6), position), (parts,), jnp.float32, smallest / len(shards), largest / len(shards))
        return jnp.repeat(jnp.exp(steps), extent[position] // parts).reshape((-1,) + (1,) * (len(extent) - position - 1))

    gain = one(*shards[0])
    for cut in shards[1:]:
        gain = gain * one(*cut)
    return gain


def scatter_about(own_key, extent, scale, most, cuts=(), kind=jnp.bfloat16):
    gain = shard_levels(own_key, extent, cuts, -0.22, 0.18) if cuts else 1.0
    result = jax.random.normal(own_key, extent, jnp.float32) * scale * gain
    return jnp.minimum(jnp.maximum(result, -most), most).astype(kind)


def setup_inputs(seed: int = 0) -> dict:
    streams_of = jax.random.split(jax.random.key(seed), 10)
    image_tokens = draw_image_tokens(jax.random.fold_in(streams_of[9], 71), 0)
    latent = scatter_about(streams_of[1], (REQ, IMG, PC), 1.0, 6.0, ((0, 128), (1, 4)), jnp.float32)
    text_memory = draw_text_memory(jax.random.fold_in(streams_of[9], 71), 0)
    text_len = draw_text_len(jax.random.fold_in(streams_of[9], 71), 0)
    timestep = touch_ends(jax.random.randint(streams_of[4], (REQ,), 1, NSTEPS + 1), jax.random.fold_in(streams_of[4], 1), 1, NSTEPS).astype(jnp.int32)
    modulation = scatter_about(streams_of[5], (REQ, 5, D), 0.6, 3.0, ((0, 128),), jnp.float32)
    projection = scatter_about(streams_of[6], (3, D, HD), (D // 2) ** -0.5, 0.21875, ((2, 4),))
    out_weight = scatter_about(streams_of[7], (HD, D), (HD // 8) ** -0.5, 0.625, ((0, 4),))
    final_weight = scatter_about(streams_of[8], (D, PC), D ** -0.5, 0.15625)
    return {"image_tokens": image_tokens, "latent": latent, "text_memory": text_memory, "text_len": text_len, "timestep": timestep, "modulation": modulation, "projection": projection, "out_weight": out_weight, "final_weight": final_weight}


eps_norm = 1e-06
shift_value = 3.0
masked_score = -1e+30
guide_scale = 7.0

def layer_norm(values):
    row_mean = lax.optimization_barrier(jnp.mean(values, axis=-1, keepdims=True))
    centred = values - row_mean
    spread = lax.optimization_barrier(jnp.mean(centred * centred, axis=-1, keepdims=True))
    return centred * lax.rsqrt(spread + eps_norm)

def sigma_of(step_index):
    fraction = step_index.astype(jnp.float32) / NSTEPS
    return shift_value * fraction / (1.0 + (shift_value - 1.0) * fraction)

def rounded(values):
    return lax.optimization_barrier(values.astype(jnp.bfloat16)).astype(jnp.float32)

def reference(image_tokens, latent, text_memory, text_len, timestep, modulation, projection, out_weight, final_weight):
    proj_full = projection.astype(jnp.float32)
    out_full = out_weight.astype(jnp.float32)
    final_full = final_weight.astype(jnp.float32)

    def one_request(pieces):
        tokens_r, memory_r, length_r, modulation_r = pieces
        features = tokens_r.astype(jnp.float32)
        modulated = rounded(layer_norm(features) * (1.0 + modulation_r[1]) + modulation_r[0])
        projected = rounded(jnp.einsum('td,cde->cte', modulated, proj_full))
        queries = projected[0].reshape(IMG, HEADS, HEAD)
        key_rows = jnp.concatenate([memory_r[0].astype(jnp.float32), projected[1]], axis=0).reshape(TXT + IMG, HEADS, HEAD)
        value_rows = jnp.concatenate([memory_r[1].astype(jnp.float32), projected[2]], axis=0).reshape(TXT + IMG, HEADS, HEAD)
        valid_keys = jnp.concatenate([jnp.arange(TXT) < length_r, jnp.ones((IMG,), dtype=bool)])
        scores = jnp.einsum('qhe,khe->qhk', queries, key_rows) / math.sqrt(HEAD)
        scores = jnp.where(valid_keys[None, None, :], scores, masked_score)
        row_top = lax.optimization_barrier(jnp.max(scores, axis=-1, keepdims=True))
        exponentials = jnp.exp(scores - row_top)
        row_sum = lax.optimization_barrier(jnp.sum(exponentials, axis=-1))
        weighted = jnp.einsum('qhk,khe->qhe', rounded(exponentials), value_rows)
        attended = rounded(weighted / row_sum[..., None]).reshape(IMG, HEADS * HEAD)
        update = jnp.dot(attended, out_full, preferred_element_type=jnp.float32)
        residual = features + modulation_r[2] * update
        final_in = rounded(layer_norm(residual) * (1.0 + modulation_r[4]) + modulation_r[3])
        return jnp.dot(final_in, final_full, preferred_element_type=jnp.float32)
    raw_velocity = lax.map(one_request, (image_tokens, text_memory, text_len, modulation))
    conditional = raw_velocity[0::2]
    unconditional = raw_velocity[1::2]
    guided = unconditional + guide_scale * (conditional - unconditional)
    velocity = jnp.repeat(guided, 2, axis=0)
    step_size = sigma_of(timestep - 1) - sigma_of(timestep)
    latent_next = latent + step_size[:, None, None] * velocity
    return (velocity, latent_next)
```

```python
import functools

import jax
import jax.numpy as jnp
from jax import lax
from jax.experimental import pallas as pl
from jax.experimental.pallas import tpu as pltpu
from jax.sharding import PartitionSpec as P

HEAD = 64
NSTEPS = 28
NX = 4
NY = 4
NZH = 4

eps_norm = 1e-06
shift_value = 3.0
masked_score = -1e30
guide_scale = 7.0
MESH = pl.DeviceIdType.MESH
BF16 = jnp.bfloat16
F32 = jnp.float32


def sigma_of(step_index):
    fraction = step_index.astype(jnp.float32) / NSTEPS
    return shift_value * fraction / (1.0 + (shift_value - 1.0) * fraction)


def normalised(values, width):
    row_mean = jnp.sum(values, axis=-1, keepdims=True) * (1.0 / width)
    centred = values - row_mean
    spread = jnp.sum(centred * centred, axis=-1, keepdims=True) * (1.0 / width)
    return centred * lax.rsqrt(spread + eps_norm)


def kernel(
    tok_in,
    text_in,
    len_in,
    mod_in,
    proj_in,
    outw_in,
    finw_in,
    vel,
    tiles,
    wproj,
    text,
    mod,
    length,
    wout,
    wfin,
    modulated,
    query,
    key_t,
    value,
    obuf,
    att,
    upd,
    vbuf,
    vrecv,
    loc_sem,
    tok_rx,
    own_tx,
    fwd_tx,
    rel_tx,
    w_rx,
    w_tx,
    small_rx,
    small_tx,
    wo_rx,
    wo_tx,
    woc_rx,
    woc_tx,
    att_rx,
    att_tx,
    v_rx,
    v_tx,
):
    rows, width = tiles.shape[1], tiles.shape[2]
    heads_width = wproj.shape[2]
    piece = rows // 4
    txt = text.shape[1]
    r = lax.axis_index("row")
    t = lax.axis_index("col")
    c = r % 2
    x = (r // 2) % NX
    y = (r // (2 * NX)) % NY
    zh = r // (2 * NX * NY)
    base = r - c
    partner = base + 1 - c
    half = t // 2
    local = c == half
    remote = c != half
    t_inner = 1 + half
    t_outer = 3 * half
    outer_i = (t - t_inner) * (t - t_inner)
    inner = outer_i == 0
    outer = outer_i == 1
    remote_i = (c - half) * (c - half)
    mate = 4 * half + 1 - t
    opp = 3 - t
    zstep = outer_i * (2 * half - 1)
    opp_row = r + ((zh + zstep + NZH) % NZH - zh) * (2 * NX * NY)
    quarter = (x % 2) + 2 * (y % 2)
    xs = 2 * (1 - 2 * (x % 2))
    ys = 2 * NX * (1 - 2 * (y % 2))
    block = [r + xs, r + ys, r + xs + ys]
    block_quarter = [
        (1 - x % 2) + 2 * (y % 2),
        (x % 2) + 2 * (1 - y % 2),
        (1 - x % 2) + 2 * (1 - y % 2),
    ]
    own_shard = t + remote_i * (3 - 2 * t)
    lane = pl.ds(pl.multiple_of(c * (width // 2), 128), width // 2)
    other_lane = pl.ds(pl.multiple_of((1 - c) * (width // 2), 128), width // 2)
    qrows = wproj.shape[1] // 4
    orows = wout.shape[1] // 4

    def here(src, dst, k):
        return pltpu.make_async_copy(src, dst, loc_sem.at[k])

    def send(src, dst, ssem, rsem, row, col):
        pltpu.make_async_remote_copy(
            src_ref=src, dst_ref=dst, send_sem=ssem, recv_sem=rsem, device_id=(row, col), device_id_type=MESH
        ).start()

    def sent(src, ssem):
        pltpu.make_async_remote_copy(
            src_ref=src, dst_ref=src, send_sem=ssem, recv_sem=ssem, device_id=(partner, t), device_id_type=MESH
        ).wait_send()

    def got(dst, rsem):
        pltpu.make_async_remote_copy(
            src_ref=dst, dst_ref=dst, send_sem=rsem, recv_sem=rsem, device_id=(partner, t), device_id_type=MESH
        ).wait_recv()

    def tok_piece(slot, p):
        return tiles.at[slot, pl.ds(pl.multiple_of(p * piece, piece), piece), :]

    def own_piece(p):
        return tok_in.at[pl.ds(p * piece, piece), :]

    def proj_part(ref, q):
        return ref.at[:, pl.ds(pl.multiple_of(q * qrows, qrows), qrows), :]

    def out_part(shard, q):
        return wout.at[shard, pl.ds(pl.multiple_of(q * orows, orows), orows), lane]

    here(outw_in, wout.at[t], 0).start()
    here(finw_in, wfin, 1).start()

    @pl.when(local)
    def _():
        here(tok_in, tiles.at[0], 2).start()
        here(proj_in, wproj, 3).start()
        here(text_in, text, 4).start()
        here(mod_in, mod, 5).start()
        here(len_in, length, 6).start()

    barrier = pltpu.get_barrier_semaphore()

    def greet(row, col):
        pl.semaphore_signal(barrier, inc=1, device_id=(row, col), device_id_type=MESH)

    greet(partner, t)
    for k in range(1, 4):
        greet(base, (t + k) % 4)
        greet(base + 1, (t + k) % 4)
    for row in block:
        greet(row, t)

    @pl.when(outer)
    def _():
        greet(opp_row, opp)

    pl.semaphore_wait(barrier, 10 + outer_i)

    order = (0, 2, 1, 3)

    @pl.when(local)
    def _():
        send(proj_part(proj_in, quarter), proj_part(wproj, quarter), w_tx.at[3], w_rx.at[quarter], opp_row, opp)
        send(mod_in, mod, small_tx.at[1], small_rx.at[1], partner, t)
        send(len_in, length, small_tx.at[2], small_rx.at[2], partner, t)
        for p in order:
            send(own_piece(p), tiles.at[1, pl.ds(p * piece, piece), :], own_tx.at[p], tok_rx.at[1, p], base + p // 2, mate)
        send(tok_in, tiles.at[0], own_tx.at[4], tok_rx.at[0, 0], partner, t)

    @pl.when(remote)
    def _():
        slot = 2 + outer_i
        for p in order:
            send(own_piece(p), tok_piece(slot, p), own_tx.at[p], tok_rx.at[slot, p], base + p // 2, 2 - half)
        send(text_in, text, small_tx.at[0], small_rx.at[0], partner, opp)

    for k in range(3):
        col = (t + 1 + k) % 4
        same = 1 - jnp.minimum((col - opp) * (col - opp), 1)
        row = r + same * (opp_row - r)
        q = quarter
        send(
            outw_in.at[pl.ds(pl.multiple_of(q * orows, orows), orows), lane],
            out_part(t, q),
            wo_tx.at[k, 3],
            wo_rx.at[t, q],
            row,
            col,
        )

    def forward(slot, p):
        ref = tok_piece(slot, p)
        j = p - 2 * c
        got(ref, tok_rx.at[slot, p])
        if slot > 1:

            @pl.when(inner)
            def _():
                send(ref, ref, rel_tx.at[slot - 2, j], tok_rx.at[slot, p], r, t_outer)

        send(ref, ref, fwd_tx.at[slot - 1, j], tok_rx.at[slot, p], partner, t)

    def project(slot):
        def chunk(i, carry):
            at = pl.ds(pl.multiple_of(i * 32, 32), 32)
            unit = normalised(tiles[slot, at, :].astype(F32), width)
            modulated[at, :] = (unit * (1.0 + mod[1:2, :]) + mod[0:1, :]).astype(BF16)
            return carry

        lax.fori_loop(0, rows // 32, chunk, 0)
        at = pl.ds(pl.multiple_of(slot * rows, rows), rows)
        m = modulated[...]
        q = jnp.dot(m, wproj[0], preferred_element_type=F32).astype(BF16)
        query[at, :] = q * jnp.bfloat16(0.125)
        k = jnp.dot(m, wproj[1], preferred_element_type=F32).astype(BF16)
        key_t[:, at] = k.T
        value[at, :] = jnp.dot(m, wproj[2], preferred_element_type=F32).astype(BF16)

    @pl.when(remote)
    def _():
        ref = proj_part(wproj, quarter)
        got(ref, w_rx.at[quarter])
        for k in range(3):
            send(ref, ref, w_tx.at[k], w_rx.at[quarter], block[k], t)

    @pl.when(local)
    def _():
        here(tok_in, tiles.at[0], 2).wait()
        here(proj_in, wproj, 3).wait()
        here(text_in, text, 4).wait()
        here(mod_in, mod, 5).wait()
        here(len_in, length, 6).wait()
        project(0)

    first, second = 2 * c, 2 * c + 1
    for p in (first, second):
        forward(1, p)
    for p in (first, second):
        forward(2, p)
        forward(3, p)

    for k in range(3):
        shard = (t + 1 + k) % 4
        ref = out_part(shard, quarter)
        got(ref, wo_rx.at[shard, quarter])
        for b in range(3):
            send(ref, ref, wo_tx.at[k, b], wo_rx.at[shard, quarter], block[b], t)

    @pl.when(remote)
    def _():
        for k in range(3):
            q = block_quarter[k]
            got(proj_part(wproj, q), w_rx.at[q])
        got(mod, small_rx.at[1])
        got(tiles.at[0], tok_rx.at[0, 0])
        project(0)

    other = 2 * (1 - c)

    def rest(slot, carry):
        for j in range(2):
            p = other + j
            got(tok_piece(slot, p), tok_rx.at[slot, p])
        project(slot)
        return carry

    lax.fori_loop(1, 4, rest, 0)

    @pl.when(remote)
    def _():
        got(text, small_rx.at[0])
        got(length, small_rx.at[2])

    for k in range(3):
        shard = (t + 1 + k) % 4
        for b in range(3):
            q = block_quarter[b]
            got(out_part(shard, q), wo_rx.at[shard, q])
        ref = wout.at[shard, :, lane]
        send(ref, ref, woc_tx.at[k], woc_rx.at[shard], partner, t)

    keys = 4 * rows
    pad = key_t.shape[1] - keys
    key_t[:, keys:] = jnp.concatenate([text[0], jnp.zeros((pad - txt, heads_width), BF16)], axis=0).T
    value[keys:, :] = jnp.concatenate([text[1], jnp.zeros((pad - txt, heads_width), BF16)], axis=0)
    valid = lax.broadcasted_iota(jnp.int32, (1, pad), 1) < length[...]
    feature = lax.broadcasted_iota(jnp.int32, (1, heads_width), 1) // HEAD

    fslot = remote_i * (3 - outer_i)

    def attend(i, carry):
        slot = (fslot + i) % 4
        at = pl.ds(pl.multiple_of(slot * rows, rows), rows)
        q_all = query[at, :]
        out = jnp.zeros((rows, heads_width), F32)
        for head in range(heads_width // HEAD):
            q = jnp.where(feature == head, q_all, jnp.zeros_like(q_all))
            s_img = jnp.dot(q, key_t[:, :keys], preferred_element_type=F32)
            s_txt = jnp.dot(q, key_t[:, keys:], preferred_element_type=F32)
            s_txt = jnp.where(valid, s_txt, masked_score)
            top = jnp.maximum(
                jnp.max(s_img, axis=-1, keepdims=True), jnp.max(s_txt, axis=-1, keepdims=True)
            )
            e_img = jnp.exp(s_img - top)
            e_txt = jnp.exp(s_txt - top)
            total = jnp.sum(e_img, axis=-1, keepdims=True) + jnp.sum(e_txt, axis=-1, keepdims=True)
            weighted = jnp.dot(e_img.astype(BF16), value[:keys, :], preferred_element_type=F32)
            weighted = weighted + jnp.dot(e_txt.astype(BF16), value[keys:, :], preferred_element_type=F32)
            out = jnp.where(feature == head, weighted / total, out)
        done = out.astype(BF16)
        dst = slot

        @pl.when(slot == fslot)
        def _():
            att[own_shard] = done

        @pl.when(slot != fslot)
        def _():
            obuf[dst] = done
            far = slot // 2
            odd = slot % 2
            col = (1 - far) * ((1 - odd) * t + odd * mate) + far * ((1 - odd) * t_outer + odd * t_inner)
            core = (1 - far) * half + far * (1 - half)
            send(obuf.at[dst], att.at[own_shard], att_tx.at[dst], att_rx.at[own_shard], base + core, col)

        return carry

    lax.fori_loop(1, 5, attend, 0)

    here(outw_in, wout.at[t], 0).wait()
    here(finw_in, wfin, 1).wait()
    for k in range(3):
        shard = (t + 1 + k) % 4
        got(wout.at[shard, :, other_lane], woc_rx.at[shard])
    upd[...] = jnp.dot(att[own_shard], wout[own_shard], preferred_element_type=F32)
    for k in range(1, 4):
        shard = (own_shard + k) % 4
        got(att.at[shard], att_rx.at[shard])
        upd[...] += jnp.dot(att[shard], wout[shard], preferred_element_type=F32)

    def last(i, carry):
        at = pl.ds(pl.multiple_of(i * 32, 32), 32)
        residual = tiles[fslot, at, :].astype(F32) + mod[2:3, :] * upd[at, :]
        unit = normalised(residual, width)
        modulated[at, :] = (unit * (1.0 + mod[4:5, :]) + mod[3:4, :]).astype(BF16)
        return carry

    lax.fori_loop(0, rows // 32, last, 0)
    raw = jnp.dot(modulated[...], wfin[...], preferred_element_type=F32)
    vbuf[...] = raw

    @pl.when(local)
    def _():
        send(vbuf, vrecv.at[half], v_tx.at[0], v_rx.at[half], partner, t)
        vel[half] = raw
        got(vrecv.at[1 - half], v_rx.at[1 - half])
        vel[1 - half] = vrecv[1 - half]
        sent(vbuf, v_tx.at[0])

    @pl.when(remote)
    def _():
        send(vbuf, vrecv.at[half], v_tx.at[0], v_rx.at[half], base, (t + 2) % 4)
        send(vbuf, vrecv.at[half], v_tx.at[1], v_rx.at[half], base + 1, (t + 2) % 4)
        for q in range(2):
            got(vrecv.at[q], v_rx.at[q])
            vel[q] = vrecv[q]
        sent(vbuf, v_tx.at[0])
        sent(vbuf, v_tx.at[1])

    for k in range(3):
        sent(out_part(t, quarter), wo_tx.at[k, 3])
        for b in range(3):
            sent(out_part(t, quarter), wo_tx.at[k, b])
        sent(wout.at[t, :, lane], woc_tx.at[k])
    for slot in range(4):

        @pl.when(slot != fslot)
        def _():
            sent(obuf.at[slot], att_tx.at[slot])

    for p in range(4):
        sent(own_piece(p), own_tx.at[p])
    for j in range(2):
        for slot in range(3):
            sent(tok_piece(1, 0), fwd_tx.at[slot, j])

        @pl.when(inner)
        def _():
            for slot in range(2):
                sent(tok_piece(1, 0), rel_tx.at[slot, j])

    @pl.when(local)
    def _():
        sent(tok_in, own_tx.at[4])
        sent(proj_part(proj_in, quarter), w_tx.at[3])
        sent(mod_in, small_tx.at[1])
        sent(len_in, small_tx.at[2])

    @pl.when(remote)
    def _():
        sent(text_in, small_tx.at[0])
        for k in range(3):
            sent(proj_part(wproj, quarter), w_tx.at[k])


def velocities(tokens, text_memory, text_len, modulation, projection, out_weight, final_weight):
    rows, width = tokens.shape
    _, txt, heads_width = text_memory.shape
    keys = 4 * rows + (txt + 127) // 128 * 128
    dma = pltpu.SemaphoreType.DMA
    return pl.pallas_call(
        kernel,
        out_shape=jax.ShapeDtypeStruct((2, rows, final_weight.shape[1]), F32),
        in_specs=[pl.BlockSpec(memory_space=pl.ANY)] * 7,
        out_specs=pl.BlockSpec(memory_space=pltpu.VMEM),
        scratch_shapes=[
            pltpu.VMEM((4, rows, width), BF16),
            pltpu.VMEM(projection.shape, BF16),
            pltpu.VMEM(text_memory.shape, BF16),
            pltpu.VMEM(modulation.shape, F32),
            pltpu.VMEM((1, 1), jnp.int32),
            pltpu.VMEM((4,) + out_weight.shape, BF16),
            pltpu.VMEM(final_weight.shape, BF16),
            pltpu.VMEM((rows, width), BF16),
            pltpu.VMEM((4 * rows, heads_width), BF16),
            pltpu.VMEM((heads_width, keys), BF16),
            pltpu.VMEM((keys, heads_width), BF16),
            pltpu.VMEM((4, rows, heads_width), BF16),
            pltpu.VMEM((4, rows, heads_width), BF16),
            pltpu.VMEM((rows, width), F32),
            pltpu.VMEM((rows, final_weight.shape[1]), F32),
            pltpu.VMEM((2, rows, final_weight.shape[1]), F32),
            dma((7,)),
            dma((4, 4)),
            dma((5,)),
            dma((3, 2)),
            dma((2, 2)),
            dma((4,)),
            dma((4,)),
            dma((3,)),
            dma((3,)),
            dma((4, 4)),
            dma((3, 4)),
            dma((4,)),
            dma((3,)),
            dma((4,)),
            dma((4,)),
            dma((2,)),
            dma((2,)),
        ],
        compiler_params=pltpu.CompilerParams(
            collective_id=0, has_side_effects=True, vmem_limit_bytes=56 * 1024 * 1024
        ),
    )(tokens, text_memory, text_len, modulation, projection, out_weight, final_weight)


def per_device(
    image_tokens,
    latent,
    text_memory,
    text_len,
    timestep,
    modulation,
    projection,
    out_weight,
    final_weight,
):
    raw = velocities(
        image_tokens[0],
        text_memory[0],
        text_len.reshape(1, 1),
        modulation[0],
        projection,
        out_weight,
        final_weight,
    )
    velocity = (raw[1] + guide_scale * (raw[0] - raw[1]))[None]
    step_size = sigma_of(timestep - 1) - sigma_of(timestep)
    latent_next = latent + step_size[:, None, None] * velocity
    return (velocity, latent_next)


def solution(mesh):
    return jax.shard_map(
        per_device,
        mesh=mesh,
        in_specs=(
            P("row", "col", None),
            P("row", "col", None),
            P("row", None, None, "col"),
            P("row"),
            P("row"),
            P("row", None, None),
            P(None, None, "col"),
            P("col", None),
            P(),
        ),
        out_specs=(P("row", "col", None), P("row", "col", None)),
        check_vma=False,
    )
```
